32 devices in a mesh: seg: 4 (over y, x), slab: 8 (over z, core).
Axes of the slice: x: 2, y: 2, z: 4, core: 2. Of those that a mesh axis runs over, the one named last changes fastest.
Arguments:
- positions: bfloat16 [4, 32, 3, 642], P('seg', 'slab'), may hold values from -6 to 6
- density: bfloat16 [4, 32, 3, 642], P('seg', 'slab'), may hold values from -6 to 6
- upsample: bfloat16 [642, 2562], replicated, may hold values from -0.25 to 0.25
- quad_weights: float32 [2562], replicated, may hold values from 0.3 to 3
- coarse_weights: float32 [642], replicated, may hold values from 0.3 to 3
- pair_target: int32 [4, 16], P('seg', 'slab'), may hold values from 0 to 3
- pair_source: int32 [4, 16], P('seg', 'slab'), may hold values from 0 to 7
- junction_cell: int32 [4, 8, 4], P('seg', 'slab'), may hold values from 0 to 3
- junction_target: int32 [4, 8, 4], P('seg', 'slab'), may hold values from 0 to 3
- wall_points: bfloat16 [4, 8, 3, 128], P('seg', 'slab'), may hold values from -6 to 6
- wall_traction: bfloat16 [4, 8, 3, 128], P('seg', 'slab'), may hold values from -6 to 6
- wall_near: int32 [4, 32, 2], P('seg', 'slab'), may hold values from 0 to 7
Outputs:
- velocity: float32 [4, 32, 3, 642], P('seg', 'slab')
The draws below stay inside these ranges and needn't reach their ends.
All inputs are finite; a program needn't handle non-finite values.
Results may differ from the reference program's by a relative error of at most 0.0024.
Values may be sent and summed in bfloat16 or wider, within the bound.
A program may use at most 64 MiB of HBM per device.

```python
import math
import jax
import jax.numpy as jnp
from jax import lax

P_SIZE = 642
Q = 2562
WP = 128
CELL_DEV = 4
HALO = 2
NEAR = 2
PAIRS_DEV = 2
CELLS_SEG = 32
PATCHES_SEG = 8
N_SEG = 4
N_SLAB = 8


def set_ends(values, key, least, top_value):
    index_at = [jax.random.randint(jax.random.fold_in(key, axis), (), 0, length) for axis, length in enumerate(values.shape)]
    widest = values.shape.index(max(values.shape))
    beside = index_at[:widest] + [(index_at[widest] + 1) % values.shape[widest]] + index_at[widest + 1:]
    return values.at[tuple(index_at)].set(least).at[tuple(beside)].set(top_value)


def block_levels(own_key, dims, pieces, smallest, top_value):
    def one(axis_at, shards_of):
        draws = jax.random.uniform(jax.random.fold_in(jax.random.fold_in(own_key, 6), axis_at), (shards_of,), jnp.float32, smallest / len(pieces), top_value / len(pieces))
        return jnp.repeat(jnp.exp(draws), dims[axis_at] // shards_of).reshape((-1,) + (1,) * (len(dims) - axis_at - 1))

    level = one(*pieces[0])
    for cut in pieces[1:]:
        level = level * one(*cut)
    return level


def scatter_about(own_key, extent, scale, limit, split=(), kind=jnp.bfloat16):
    values = jax.random.normal(own_key, extent, jnp.float32) * scale
    if len(split) > 0:
        values = block_levels(own_key, extent, split, -0.22, 0.18) * values
    return jnp.clip(values, min=-limit, max=limit).astype(kind)


def setup_inputs(seed: int = 0) -> dict:
    key_list = jax.random.split(jax.random.key(seed), 13)
    return {
        "positions": scatter_about(key_list[0], (N_SEG, CELLS_SEG, 3, P_SIZE), 1.0, 6.0, ((0, 4), (1, 8))),
        "density": scatter_about(key_list[1], (N_SEG, CELLS_SEG, 3, P_SIZE), 1.0, 6.0, ((0, 4), (1, 8))),
        "upsample": scatter_about(key_list[2], (P_SIZE, Q), P_SIZE ** -0.5, 0.25),
        "quad_weights": jnp.clip(jnp.exp(jax.random.uniform(key_list[3], (Q,), jnp.float32, math.log(0.3), math.log(3.0))), 0.3, 3.0),
        "coarse_weights": jnp.clip(jnp.exp(jax.random.uniform(key_list[4], (P_SIZE,), jnp.float32, math.log(0.3), math.log(3.0))), 0.3, 3.0),
        "pair_target": set_ends(jax.random.randint(key_list[5], (N_SEG, N_SLAB * PAIRS_DEV), 0, CELL_DEV), jax.random.fold_in(key_list[5], 1), 0, CELL_DEV - 1).astype(jnp.int32),
        "pair_source": set_ends(jax.random.randint(key_list[6], (N_SEG, N_SLAB * PAIRS_DEV), 0, CELL_DEV + 2 * HALO), jax.random.fold_in(key_list[6], 1), 0, (CELL_DEV + 2 * HALO) - 1).astype(jnp.int32),
        "junction_cell": set_ends(jax.random.randint(key_list[7], (N_SEG, N_SLAB, N_SEG), 0, CELL_DEV), jax.random.fold_in(key_list[7], 1), 0, CELL_DEV - 1).astype(jnp.int32),
        "junction_target": set_ends(jax.random.randint(key_list[8], (N_SEG, N_SLAB, N_SEG), 0, CELL_DEV), jax.random.fold_in(key_list[8], 1), 0, CELL_DEV - 1).astype(jnp.int32),
        "wall_points": scatter_about(key_list[9], (N_SEG, PATCHES_SEG, 3, WP), 1.0, 6.0, ((0, 4), (1, 8))),
        "wall_traction": scatter_about(key_list[10], (N_SEG, PATCHES_SEG, 3, WP), 1.0, 6.0, ((0, 4), (1, 8))),
        "wall_near": set_ends(jax.random.randint(key_list[11], (N_SEG, CELLS_SEG, NEAR), 0, PATCHES_SEG), jax.random.fold_in(key_list[11], 1), 0, PATCHES_SEG - 1).astype(jnp.int32),
    }


EPSILON2 = 0.05
WALL_GAIN = 3.0

def kernel_rows(targets, sources, strength):
    offset = targets[:, :, None] - sources[:, None, :]
    distance2 = lax.optimization_barrier(jnp.sum(offset * offset, axis=0))
    inverse = lax.rsqrt(distance2 + EPSILON2)
    inverse3 = inverse * inverse * inverse
    along_offset = lax.optimization_barrier(jnp.sum(offset * strength[:, None, :], axis=0))
    summand = (strength[:, None, :] * (distance2 + 2.0 * EPSILON2) + along_offset[None] * offset) * inverse3[None]
    return lax.optimization_barrier(jnp.sum(summand, axis=2)) / (8.0 * math.pi)

def grouped(func, operands, group):
    total = operands[0].shape[0]
    shaped = jax.tree.map(lambda leaf_array: leaf_array.reshape((total // group, group) + leaf_array.shape[1:]), operands)
    result = lax.map(lambda batch: jax.vmap(func)(*batch), shaped)
    return result.reshape((total,) + result.shape[2:])

def reference(positions, density, upsample, quad_weights, coarse_weights, pair_target, pair_source, junction_cell, junction_target, wall_points, wall_traction, wall_near):
    cell_seg = N_SLAB * CELL_DEV
    upsample_full = upsample.astype(jnp.float32)
    fine_points = jnp.einsum('gckp,pq->gckq', positions.astype(jnp.float32), upsample_full, precision=lax.Precision.HIGHEST).astype(jnp.bfloat16)
    fine_density = jnp.einsum('gckp,pq->gckq', density.astype(jnp.float32), upsample_full, precision=lax.Precision.HIGHEST).astype(jnp.bfloat16)
    velocity = jnp.zeros(positions.shape, jnp.float32)
    slab_of = jnp.arange(N_SLAB * PAIRS_DEV, dtype=jnp.int32) // PAIRS_DEV
    target_cell = (slab_of[None, :] * CELL_DEV + pair_target).reshape(-1)
    source_cell = (slab_of[None, :] * CELL_DEV - HALO + pair_source).reshape(-1)
    inside = ((source_cell >= 0) & (source_cell < cell_seg)).astype(jnp.float32)
    source_clip = jnp.clip(source_cell, 0, cell_seg - 1).astype(jnp.int32)
    segment_of = jnp.broadcast_to(jnp.arange(N_SEG, dtype=jnp.int32)[:, None], pair_target.shape).reshape(-1)

    def fine_pair(target_pts, source_pts, source_den, weight_inside):
        strength = source_den.astype(jnp.float32) * quad_weights[None, :]
        return kernel_rows(target_pts.astype(jnp.float32), source_pts.astype(jnp.float32), strength) * weight_inside
    blocks = grouped(fine_pair, (positions[segment_of, target_cell], fine_points[segment_of, source_clip], fine_density[segment_of, source_clip], inside), 4)
    velocity = velocity.at[segment_of, target_cell].add(blocks)
    source_seg, slab_index, target_seg = jnp.meshgrid(jnp.arange(N_SEG, dtype=jnp.int32), jnp.arange(N_SLAB, dtype=jnp.int32), jnp.arange(N_SEG, dtype=jnp.int32), indexing='ij')
    junction_source = (slab_index * CELL_DEV + junction_cell).reshape(-1)
    junction_goal = (slab_index * CELL_DEV + junction_target[target_seg, slab_index, source_seg]).reshape(-1)
    alive_mask = (source_seg != target_seg).astype(jnp.float32).reshape(-1)
    source_seg = source_seg.reshape(-1)
    target_seg = target_seg.reshape(-1)

    def coarse_pair(target_pts, source_pts, source_den, weight_alive):
        strength = source_den.astype(jnp.float32) * coarse_weights[None, :]
        return kernel_rows(target_pts.astype(jnp.float32), source_pts.astype(jnp.float32), strength) * weight_alive
    junction_blocks = grouped(coarse_pair, (positions[target_seg, junction_goal], positions[source_seg, junction_source], density[source_seg, junction_source], alive_mask), 4)
    velocity = velocity.at[target_seg, junction_goal].add(junction_blocks)
    wall_seg = jnp.broadcast_to(jnp.arange(N_SEG, dtype=jnp.int32)[:, None, None], wall_near.shape).reshape(-1)
    wall_cell = jnp.broadcast_to(jnp.arange(cell_seg, dtype=jnp.int32)[None, :, None], wall_near.shape).reshape(-1)
    wall_patch = wall_near.reshape(-1)

    def wall_pair(target_pts, source_pts, source_den):
        return kernel_rows(target_pts.astype(jnp.float32), source_pts.astype(jnp.float32), source_den.astype(jnp.float32) * WALL_GAIN)
    wall_blocks = grouped(wall_pair, (positions[wall_seg, wall_cell], wall_points[wall_seg, wall_patch], wall_traction[wall_seg, wall_patch]), 4)
    velocity = velocity.at[wall_seg, wall_cell].add(wall_blocks)
    return velocity
```

```python
import functools
import math

import jax
import jax.numpy as jnp
from jax import lax
from jax.experimental import pallas as pl
from jax.experimental.pallas import tpu as pltpu
from jax.sharding import PartitionSpec as P

MESH = pl.DeviceIdType.MESH
HALO = 2
EPSILON2 = 0.05
WALL_GAIN = 3.0
LANES = 128
TERMS = 16
KAPPA = 1.0 / EPSILON2
F32 = jnp.float32
BF16 = jnp.bfloat16


def up(n, m):
    return -(-n // m) * m


def split(value, parts):
    out = []
    for _ in range(parts):
        piece = value.astype(BF16).astype(F32)
        out.append(piece)
        value = value - piece
    return out


def kernel(
    cfg,
    pair_target, pair_source, junction_cell, junction_target, wall_near,
    positions, density, upsample, quad, coarse, wall_points, wall_traction,
    out,
    own, cells, jsend, jrecv, walls, ups, rows, lhs, fine, ysrc, gsrc, yd, yg, ga, gb, xt, acc,
    local_sem, halo_send, halo_recv, junction_send, junction_recv, wall_send, wall_recv,
):
    count, points, fine_points, pairs, near, patch, segs, slabs, per_slab = cfg
    pt, qp = up(points, LANES), up(fine_points, LANES)
    rows_t = up(points, 16)
    seg, slab = lax.axis_index("seg"), lax.axis_index("slab")

    copies = [
        pltpu.make_async_copy(positions.at[0], cells.at[pl.ds(HALO, count), 0], local_sem.at[0]),
        pltpu.make_async_copy(density.at[0], cells.at[pl.ds(HALO, count), 1], local_sem.at[1]),
        pltpu.make_async_copy(wall_points.at[0], walls.at[pl.ds(slab * per_slab, per_slab), 0], local_sem.at[2]),
        pltpu.make_async_copy(wall_traction.at[0], walls.at[pl.ds(slab * per_slab, per_slab), 1], local_sem.at[3]),
    ]
    home = [
        pltpu.make_async_copy(positions.at[0], own.at[0], local_sem.at[5]),
        pltpu.make_async_copy(density.at[0], own.at[1], local_sem.at[6]),
    ]
    big = pltpu.make_async_copy(upsample, ups, local_sem.at[4])
    for copy in home + copies:
        copy.start()
    big.start()

    barrier = pltpu.get_barrier_semaphore()
    for o in range(1, segs):
        pl.semaphore_signal(barrier, inc=1, device_id={"seg": lax.rem(seg + o, segs)}, device_id_type=MESH)
    for o in range(1, slabs):
        pl.semaphore_signal(barrier, inc=1, device_id={"slab": lax.rem(slab + o, slabs)}, device_id_type=MESH)

    for copy in home + copies:
        copy.wait()
    for b in range(segs):
        jsend[b, 0] = own[0, junction_cell[0, 0, b]]
        jsend[b, 1] = own[1, junction_cell[0, 0, b]]
    ysrc[...] = jnp.zeros_like(ysrc)
    gsrc[...] = jnp.zeros_like(gsrc)

    @pl.when(slab == 0)
    def _():
        cells[0:HALO] = jnp.zeros((HALO,) + cells.shape[1:], BF16)

    @pl.when(slab == slabs - 1)
    def _():
        cells[HALO + count:] = jnp.zeros((HALO,) + cells.shape[1:], BF16)

    pl.semaphore_wait(barrier, segs - 1 + slabs - 1)

    def halo_up():
        return pltpu.make_async_remote_copy(
            cells.at[pl.ds(count, HALO)], cells.at[pl.ds(0, HALO)], halo_send.at[0], halo_recv.at[0],
            device_id={"slab": lax.rem(slab + 1, slabs)}, device_id_type=MESH)

    def halo_down():
        return pltpu.make_async_remote_copy(
            cells.at[pl.ds(HALO, HALO)], cells.at[pl.ds(HALO + count, HALO)], halo_send.at[1], halo_recv.at[1],
            device_id={"slab": lax.rem(slab + slabs - 1, slabs)}, device_id_type=MESH)

    def junction(o):
        return pltpu.make_async_remote_copy(
            jsend.at[lax.rem(seg + o, segs)], jrecv.at[seg], junction_send.at[o], junction_recv.at[o],
            device_id={"seg": lax.rem(seg + o, segs)}, device_id_type=MESH)

    def junction_in(o):
        return pltpu.make_async_remote_copy(
            jsend.at[seg], jrecv.at[lax.rem(seg + segs - o, segs)], junction_send.at[o], junction_recv.at[o],
            device_id={"seg": lax.rem(seg + o, segs)}, device_id_type=MESH)

    def wall(o, of):
        slot = pl.ds(of * per_slab, per_slab)
        return pltpu.make_async_remote_copy(
            walls.at[slot], walls.at[slot], wall_send.at[o], wall_recv.at[o],
            device_id={"slab": lax.rem(slab + o, slabs)}, device_id_type=MESH)

    @pl.when(slab < slabs - 1)
    def _():
        halo_up().start()

    @pl.when(slab > 0)
    def _():
        halo_down().start()

    for o in range(1, segs):
        junction(o).start()
    for o in range(slabs - 1, 0, -1):
        wall(o, slab).start()

    rows[...] = jnp.zeros_like(rows)
    for c in range(count):
        x = own[0, c].astype(F32)
        rows[0:3, 0:points] = x
        rows[3:6, 0:points] = x
        for i, piece in enumerate(split(KAPPA * jnp.sum(x * x, axis=0, keepdims=True), 3)):
            rows[6 + i:7 + i, 0:points] = piece
        rows[9:12, 0:points] = jnp.ones((3, points), F32)
        xt[c] = rows[...].T[0:rows_t].astype(BF16)
        acc[c] = jnp.zeros(acc.shape[1:], F32)

    def prepare(start, size):
        at = pl.ds(start, size)
        y, g = ysrc[0:3, at], gsrc[0:3, at]
        g_hi, g_lo = split(g, 2)
        y_hi, y_lo = split((-2.0 * KAPPA) * y, 2)
        norm = split(KAPPA * jnp.sum(y * y, axis=0, keepdims=True) + 1.0, 3)
        dot = split(-jnp.sum(y * (g_hi + g_lo), axis=0, keepdims=True), 3)
        one = jnp.ones((3, size), F32)
        none = jnp.zeros((3, size), F32)
        pad = jnp.zeros((TERMS - 12, size), F32)
        yd[:, at] = jnp.concatenate([y_hi, y_lo, one] + norm + [pad], axis=0).astype(BF16)
        yg[:, at] = jnp.concatenate([g_hi, g_lo, none] + dot + [pad], axis=0).astype(BF16)
        ga[:, at] = jnp.concatenate([one[0:1], y, jnp.zeros((TERMS - 4, size), F32)], axis=0).astype(BF16)
        gb[:, at] = jnp.concatenate([jnp.zeros((TERMS - 8, size), F32), g_hi, g_lo, none[0:2]], axis=0).astype(BF16)

    def chunk(targets, start):
        at = pl.ds(pl.multiple_of(start, LANES), LANES)
        first = jnp.dot(
            targets, jnp.concatenate([yd[:, at], yg[:, at]], axis=1), preferred_element_type=F32)
        inverse = lax.rsqrt(first[:, :LANES])
        inverse3 = inverse * inverse * inverse
        along = (first[:, LANES:] * inverse3).astype(BF16)
        plain = (inverse + inverse3).astype(BF16)
        return lax.dot_general(
            jnp.concatenate([ga[:, at], gb[:, at]], axis=1),
            jnp.concatenate([along, plain], axis=1),
            (((1,), (1,)), ((), ())), preferred_element_type=F32)

    def block(target, start, chunks):
        targets = xt[target]
        unroll = 3 if chunks % 3 == 0 else (2 if chunks % 2 == 0 else 1)

        def step(i, total):
            for u in range(unroll):
                total = total + chunk(targets, start + (i * unroll + u) * LANES)
            return total

        zero = jnp.zeros((TERMS, rows_t), F32)
        if chunks == unroll:
            return step(0, zero)
        return lax.fori_loop(0, chunks // unroll, step, zero)

    def add(target, value):
        for c in range(count):
            acc[c] = acc[c] + jnp.where(target == c, 1.0, 0.0) * value

    @pl.when(slab > 0)
    def _():
        halo_up().wait_recv()

    @pl.when(slab < slabs - 1)
    def _():
        halo_down().wait_recv()

    for k in range(pairs):
        source = cells[pair_source[0, k]]
        lhs[6 * k:6 * k + 3] = source[0].astype(F32)
        lhs[6 * k + 3:6 * k + 6] = source[1].astype(F32)
    big.wait()
    fine[...] = jnp.dot(lhs[...].astype(BF16), ups[...], preferred_element_type=F32).astype(BF16).astype(F32)
    for k in range(pairs):
        ysrc[0:3, pl.ds(k * qp, fine_points)] = fine[6 * k:6 * k + 3]
        gsrc[0:3, pl.ds(k * qp, fine_points)] = fine[6 * k + 3:6 * k + 6] * quad[...]
    prepare(0, pairs * qp)
    for k in range(pairs):
        target = pair_target[0, k]
        add(target, block(target, k * qp, qp // LANES))

    base = pairs * qp
    for o in range(1, segs):
        junction_in(o).wait_recv()
        source = jrecv[lax.rem(seg + segs - o, segs)]
        at = pl.ds(base + (o - 1) * pt, points)
        ysrc[0:3, at] = source[0].astype(F32)
        gsrc[0:3, at] = source[1].astype(F32) * coarse[...]
    prepare(base, (segs - 1) * pt)
    for o in range(1, segs):
        target = junction_target[0, 0, lax.rem(seg + segs - o, segs)]
        add(target, block(target, base + (o - 1) * pt, pt // LANES))

    base = base + (segs - 1) * pt
    for o in range(1, slabs):
        wall(o, lax.rem(slab + slabs - o, slabs)).wait_recv()
    width = up(patch, LANES)
    for c in range(count):
        for n in range(near):
            source = walls[wall_near[0, c, n]]
            at = pl.ds(base + (c * near + n) * width, patch)
            ysrc[0:3, at] = source[0].astype(F32)
            gsrc[0:3, at] = source[1].astype(F32) * WALL_GAIN
    prepare(base, count * near * width)
    scale = 1.0 / (math.sqrt(EPSILON2) * 8.0 * math.pi)
    for c in range(count):
        total = (acc[c] + block(c, base + c * near * width, near * width // LANES))[:, 0:points]
        x = own[0, c].astype(F32)
        out[0, c] = scale * (total[8:11] + total[11:14] + KAPPA * (x * total[0:1] - total[1:4]))

    @pl.when(slab < slabs - 1)
    def _():
        halo_up().wait_send()

    @pl.when(slab > 0)
    def _():
        halo_down().wait_send()

    for o in range(1, segs):
        junction(o).wait_send()
    for o in range(1, slabs):
        wall(o, slab).wait_send()


def local(segs, slabs, positions, density, upsample, quad_weights, coarse_weights, pair_target, pair_source,
          junction_cell, junction_target, wall_points, wall_traction, wall_near):
    count, points = positions.shape[1], positions.shape[3]
    fine_points = upsample.shape[1]
    pairs, near = pair_target.shape[1], wall_near.shape[2]
    per_slab, patch = wall_points.shape[1], wall_points.shape[3]
    cfg = (count, points, fine_points, pairs, near, patch, segs, slabs, per_slab)
    pt, qp = up(points, LANES), up(fine_points, LANES)
    lanes = pairs * qp + (segs - 1) * pt + count * near * up(patch, LANES)
    smem = pl.BlockSpec(memory_space=pltpu.SMEM)
    vmem = pl.BlockSpec(memory_space=pltpu.VMEM)
    far = pl.BlockSpec(memory_space=pl.ANY)
    dma = pltpu.SemaphoreType.DMA
    return pl.pallas_call(
        functools.partial(kernel, cfg),
        out_shape=jax.ShapeDtypeStruct(positions.shape, F32),
        in_specs=[smem] * 5 + [far, far, far, vmem, vmem, far, far],
        out_specs=vmem,
        scratch_shapes=[
            pltpu.VMEM((2,) + positions.shape[1:], BF16),
            pltpu.VMEM((count + 2 * HALO, 2, 3, points), BF16),
            pltpu.VMEM((segs, 2, 3, points), BF16),
            pltpu.VMEM((segs, 2, 3, points), BF16),
            pltpu.VMEM((slabs * per_slab, 2, 3, patch), BF16),
            pltpu.VMEM(upsample.shape, BF16),
            pltpu.VMEM((TERMS, pt), F32),
            pltpu.VMEM((6 * pairs, points), F32),
            pltpu.VMEM((6 * pairs, fine_points), F32),
            pltpu.VMEM((8, lanes), F32),
            pltpu.VMEM((8, lanes), F32),
            pltpu.VMEM((TERMS, lanes), BF16),
            pltpu.VMEM((TERMS, lanes), BF16),
            pltpu.VMEM((TERMS, lanes), BF16),
            pltpu.VMEM((TERMS, lanes), BF16),
            pltpu.VMEM((count, up(points, 16), TERMS), BF16),
            pltpu.VMEM((count, TERMS, up(points, 16)), F32),
            dma((7,)), dma((2,)), dma((2,)), dma((segs,)), dma((segs,)), dma((slabs,)), dma((slabs,)),
        ],
        compiler_params=pltpu.CompilerParams(collective_id=0, has_side_effects=True),
    )(pair_target, pair_source, junction_cell, junction_target, wall_near,
      positions, density, upsample, quad_weights[None], coarse_weights[None], wall_points, wall_traction)


def solution(mesh):
    placed = (
        P("seg", "slab", None, None),
        P("seg", "slab", None, None),
        P(),
        P(),
        P(),
        P("seg", "slab"),
        P("seg", "slab"),
        P("seg", "slab", None),
        P("seg", "slab", None),
        P("seg", "slab", None, None),
        P("seg", "slab", None, None),
        P("seg", "slab", None),
    )
    body = functools.partial(local, mesh.shape["seg"], mesh.shape["slab"])
    return jax.shard_map(
        body, mesh=mesh, in_specs=placed, out_specs=P("seg", "slab", None, None), check_vma=False
    )
```

```python
import functools
import math

import jax
import jax.numpy as jnp
from jax import lax
from jax.experimental import pallas as pl
from jax.experimental.pallas import tpu as pltpu
from jax.sharding import PartitionSpec as P

MESH = pl.DeviceIdType.MESH
HALO = 2
EPSILON2 = 0.05
WALL_GAIN = 3.0
LANES = 128
TERMS = 16
KAPPA = 1.0 / EPSILON2
F32 = jnp.float32
BF16 = jnp.bfloat16


def up(n, m):
    return -(-n // m) * m


def split(value, parts):
    out = []
    for _ in range(parts):
        piece = value.astype(BF16).astype(F32)
        out.append(piece)
        value = value - piece
    return out


def kernel(
    cfg,
    pair_target, pair_source, junction_cell, junction_target, wall_near,
    positions, density, upsample, quad, coarse, wall_points, wall_traction,
    out,
    own, low, high, jsend, jrecv, walls, ups, rows, lhs, fine, ysrc, gsrc, yd, yg, ga, gb, xt, xs, wide, acc,
    local_sem, halo_send, halo_recv, junction_send, junction_recv, wall_send, wall_recv,
):
    count, points, fine_points, pairs, near, patch, segs, slabs, per_slab = cfg
    pt, qp = up(points, LANES), up(fine_points, LANES)
    rows_t = up(points, 16)
    seg, slab = lax.axis_index("seg"), lax.axis_index("slab")

    copies = [
        pltpu.make_async_copy(positions.at[0], own.at[0], local_sem.at[0]),
        pltpu.make_async_copy(density.at[0], own.at[1], local_sem.at[1]),
        pltpu.make_async_copy(wall_points.at[0], walls.at[pl.ds(slab * per_slab, per_slab), 0], local_sem.at[2]),
        pltpu.make_async_copy(wall_traction.at[0], walls.at[pl.ds(slab * per_slab, per_slab), 1], local_sem.at[3]),
    ]
    big = pltpu.make_async_copy(upsample, ups, local_sem.at[4])
    for copy in copies:
        copy.start()
    big.start()

    barrier = pltpu.get_barrier_semaphore()
    for o in range(1, segs):
        pl.semaphore_signal(barrier, inc=1, device_id={"seg": lax.rem(seg + o, segs)}, device_id_type=MESH)
    for o in range(1, slabs):
        pl.semaphore_signal(barrier, inc=1, device_id={"slab": lax.rem(slab + o, slabs)}, device_id_type=MESH)

    for copy in copies:
        copy.wait()
    cell_at = lax.broadcasted_iota(jnp.int32, (count, points), 0)

    def pick(kind, i, near_by):
        total = jnp.zeros((count, points), F32)
        for ref, first in near_by:
            total = total + jnp.where(cell_at == first, ref[kind, i].astype(F32), 0.0)
        return jnp.sum(total, axis=0, keepdims=True)

    for b in range(segs):
        mine = junction_cell[0, 0, b]
        jsend[b] = jnp.concatenate(
            [pick(kind, i, [(own, mine)]) for kind in range(2) for i in range(3)], axis=0).astype(BF16)
    ysrc[...] = jnp.zeros_like(ysrc)
    gsrc[...] = jnp.zeros_like(gsrc)

    @pl.when(slab == 0)
    def _():
        low[...] = jnp.zeros_like(low)

    @pl.when(slab == slabs - 1)
    def _():
        high[...] = jnp.zeros_like(high)

    pl.semaphore_wait(barrier, segs - 1 + slabs - 1)

    def halo_up():
        return pltpu.make_async_remote_copy(
            own, low, halo_send.at[0], halo_recv.at[0],
            device_id={"slab": lax.rem(slab + 1, slabs)}, device_id_type=MESH)

    def halo_down():
        return pltpu.make_async_remote_copy(
            own, high, halo_send.at[1], halo_recv.at[1],
            device_id={"slab": lax.rem(slab + slabs - 1, slabs)}, device_id_type=MESH)

    def junction(o):
        return pltpu.make_async_remote_copy(
            jsend.at[lax.rem(seg + o, segs)], jrecv.at[seg], junction_send.at[o], junction_recv.at[o],
            device_id={"seg": lax.rem(seg + o, segs)}, device_id_type=MESH)

    def junction_in(o):
        return pltpu.make_async_remote_copy(
            jsend.at[seg], jrecv.at[lax.rem(seg + segs - o, segs)], junction_send.at[o], junction_recv.at[o],
            device_id={"seg": lax.rem(seg + o, segs)}, device_id_type=MESH)

    def wall(o, of):
        slot = pl.ds(of * per_slab, per_slab)
        return pltpu.make_async_remote_copy(
            walls.at[slot], walls.at[slot], wall_send.at[o], wall_recv.at[o],
            device_id={"slab": lax.rem(slab + o, slabs)}, device_id_type=MESH)

    @pl.when(slab < slabs - 1)
    def _():
        halo_up().start()

    @pl.when(slab > 0)
    def _():
        halo_down().start()

    for o in range(1, segs):
        junction(o).start()
    for o in range(slabs - 1, 0, -1):
        wall(o, slab).start()

    rows[...] = jnp.zeros_like(rows)
    coords = [own[0, i].astype(F32) for i in range(3)]
    norms = split(KAPPA * (coords[0] * coords[0] + coords[1] * coords[1] + coords[2] * coords[2]), 3)
    rows[9:12, 0:points] = jnp.ones((3, points), F32)
    for c in range(count):
        for i in range(3):
            line = coords[i][c:c + 1]
            xs[c, i:i + 1] = line
            rows[i:i + 1, 0:points] = line
            rows[3 + i:4 + i, 0:points] = line
            rows[6 + i:7 + i, 0:points] = norms[i][c:c + 1]
        turned = rows[...].T[0:rows_t]
        xt[c] = turned.astype(BF16)
        for i in range(3):
            wide[c, i] = jnp.broadcast_to(turned[:, i:i + 1], (rows_t, LANES))
        acc[c] = jnp.zeros(acc.shape[1:], F32)

    def prepare(start, size):
        at = pl.ds(start, size)
        y, g = ysrc[0:3, at], gsrc[0:3, at]
        g_hi, g_lo = split(g, 2)
        y_hi, y_lo = split((-2.0 * KAPPA) * y, 2)
        norm = split(KAPPA * jnp.sum(y * y, axis=0, keepdims=True) + 1.0, 3)
        dot = -jnp.sum(y * (g_hi + g_lo), axis=0, keepdims=True)
        gsrc[0:3, at] = g_hi + g_lo
        gsrc[3:4, at] = dot
        dot = split(dot, 3)
        one = jnp.ones((3, size), F32)
        none = jnp.zeros((3, size), F32)
        pad = jnp.zeros((TERMS - 12, size), F32)
        yd[:, at] = jnp.concatenate([y_hi, y_lo, one] + norm + [pad], axis=0).astype(BF16)
        yg[:, at] = jnp.concatenate([g_hi, g_lo, none] + dot + [pad], axis=0).astype(BF16)
        ga[:, at] = jnp.concatenate([one[0:1], y, jnp.zeros((TERMS - 4, size), F32)], axis=0).astype(BF16)
        gb[:, at] = jnp.concatenate([jnp.zeros((TERMS - 8, size), F32), g_hi, g_lo, none[0:2]], axis=0).astype(BF16)

    def finish(distance, along, at):
        inverse = lax.rsqrt(distance)
        inverse3 = inverse * inverse * inverse
        return lax.dot_general(
            jnp.concatenate([ga[:, at], gb[:, at]], axis=1),
            jnp.concatenate([(along * inverse3).astype(BF16), (inverse + inverse3).astype(BF16)], axis=1),
            (((1,), (1,)), ((), ())), preferred_element_type=F32)

    def group(target, start, size):
        targets = xt[target]
        ats = [pl.ds(pl.multiple_of(start + i * LANES, LANES), LANES) for i in range(size)]
        total = None
        for i in range(0, size - 1, 2):
            pair = jnp.dot(
                targets, jnp.concatenate([yd[:, ats[i]], yd[:, ats[i + 1]]], axis=1), preferred_element_type=F32)
            for at, distance in ((ats[i], pair[:, :LANES]), (ats[i + 1], pair[:, LANES:])):
                along = gsrc[3:4, at] + wide[target, 0] * gsrc[0:1, at]
                along = along + wide[target, 1] * gsrc[1:2, at]
                along = along + wide[target, 2] * gsrc[2:3, at]
                term = finish(distance, along, at)
                total = term if total is None else total + term
        if size % 2:
            at = ats[-1]
            both = jnp.dot(
                targets, jnp.concatenate([yd[:, at], yg[:, at]], axis=1), preferred_element_type=F32)
            term = finish(both[:, :LANES], both[:, LANES:], at)
            total = term if total is None else total + term
        return total

    def block(target, start, chunks):
        size = 3 if chunks % 3 == 0 else (2 if chunks % 2 == 0 else 1)

        def step(i, total):
            return total + group(target, start + i * size * LANES, size)

        if chunks == size:
            return group(target, start, size)
        return lax.fori_loop(0, chunks // size, step, jnp.zeros((TERMS, rows_t), F32))

    def add(target, value):
        for c in range(count):
            acc[c] = acc[c] + jnp.where(target == c, 1.0, 0.0) * value

    @pl.when(slab > 0)
    def _():
        halo_up().wait_recv()

    @pl.when(slab < slabs - 1)
    def _():
        halo_down().wait_recv()

    for k in range(pairs):
        source = pair_source[0, k]
        around = [(low, source + (count - HALO)), (own, source - HALO), (high, source - (HALO + count))]
        for kind in range(2):
            for i in range(3):
                lhs[6 * k + 3 * kind + i:6 * k + 3 * kind + i + 1] = pick(kind, i, around)
    big.wait()
    fine[...] = jnp.dot(lhs[...].astype(BF16), ups[...], preferred_element_type=F32).astype(BF16).astype(F32)
    for k in range(pairs):
        ysrc[0:3, pl.ds(k * qp, fine_points)] = fine[6 * k:6 * k + 3]
        gsrc[0:3, pl.ds(k * qp, fine_points)] = fine[6 * k + 3:6 * k + 6] * quad[...][None]
    prepare(0, pairs * qp)
    for k in range(pairs):
        target = pair_target[0, k]
        add(target, block(target, k * qp, qp // LANES))

    base = pairs * qp
    for o in range(1, segs):
        junction_in(o).wait_recv()
        source = jrecv[lax.rem(seg + segs - o, segs)]
        at = pl.ds(base + (o - 1) * pt, points)
        ysrc[0:3, at] = source[0:3].astype(F32)
        gsrc[0:3, at] = source[3:6].astype(F32) * coarse[...][None]
    prepare(base, (segs - 1) * pt)
    for o in range(1, segs):
        target = junction_target[0, 0, lax.rem(seg + segs - o, segs)]
        add(target, block(target, base + (o - 1) * pt, pt // LANES))

    base = base + (segs - 1) * pt
    for o in range(1, slabs):
        wall(o, lax.rem(slab + slabs - o, slabs)).wait_recv()
    width = up(patch, LANES)
    for c in range(count):
        for n in range(near):
            source = walls[wall_near[0, n, c]]
            at = pl.ds(base + (c * near + n) * width, patch)
            ysrc[0:3, at] = source[0].astype(F32)
            gsrc[0:3, at] = source[1].astype(F32) * WALL_GAIN
    prepare(base, count * near * width)
    scale = 1.0 / (math.sqrt(EPSILON2) * 8.0 * math.pi)
    for c in range(count):
        total = (acc[c] + block(c, base + c * near * width, near * width // LANES))[:, 0:points]
        x = xs[c, 0:3]
        value = scale * (total[8:11] + total[11:14] + KAPPA * (x * total[0:1] - total[1:4]))
        for i in range(3):
            out[0, i, c:c + 1] = value[i:i + 1]

    @pl.when(slab < slabs - 1)
    def _():
        halo_up().wait_send()

    @pl.when(slab > 0)
    def _():
        halo_down().wait_send()

    for o in range(1, segs):
        junction(o).wait_send()
    for o in range(1, slabs):
        wall(o, slab).wait_send()


def local(segs, slabs, positions, density, upsample, quad_weights, coarse_weights, pair_target, pair_source,
          junction_cell, junction_target, wall_points, wall_traction, wall_near):
    count, points = positions.shape[1], positions.shape[3]
    turned = (1, 3, count, points)
    fine_points = upsample.shape[1]
    pairs, near = pair_target.shape[1], wall_near.shape[2]
    per_slab, patch = wall_points.shape[1], wall_points.shape[3]
    cfg = (count, points, fine_points, pairs, near, patch, segs, slabs, per_slab)
    pt, qp = up(points, LANES), up(fine_points, LANES)
    lanes = pairs * qp + (segs - 1) * pt + count * near * up(patch, LANES)
    smem = pl.BlockSpec(memory_space=pltpu.SMEM)
    vmem = pl.BlockSpec(memory_space=pltpu.VMEM)
    far = pl.BlockSpec(memory_space=pl.ANY)
    dma = pltpu.SemaphoreType.DMA
    result = pl.pallas_call(
        functools.partial(kernel, cfg),
        out_shape=jax.ShapeDtypeStruct(turned, F32),
        in_specs=[smem] * 5 + [far, far, far, vmem, vmem, far, far],
        out_specs=vmem,
        scratch_shapes=[
            pltpu.VMEM((2,) + turned[1:], BF16),
            pltpu.VMEM((2,) + turned[1:], BF16),
            pltpu.VMEM((2,) + turned[1:], BF16),
            pltpu.VMEM((segs, 6, points), BF16),
            pltpu.VMEM((segs, 6, points), BF16),
            pltpu.VMEM((slabs * per_slab, 2, 3, patch), BF16),
            pltpu.VMEM(upsample.shape, BF16),
            pltpu.VMEM((TERMS, pt), F32),
            pltpu.VMEM((6 * pairs, points), F32),
            pltpu.VMEM((6 * pairs, fine_points), F32),
            pltpu.VMEM((8, lanes), F32),
            pltpu.VMEM((8, lanes), F32),
            pltpu.VMEM((TERMS, lanes), BF16),
            pltpu.VMEM((TERMS, lanes), BF16),
            pltpu.VMEM((TERMS, lanes), BF16),
            pltpu.VMEM((TERMS, lanes), BF16),
            pltpu.VMEM((count, up(points, 16), TERMS), BF16),
            pltpu.VMEM((count, 3, points), F32),
            pltpu.VMEM((count, 3, up(points, 16), LANES), F32),
            pltpu.VMEM((count, TERMS, up(points, 16)), F32),
            dma((5,)), dma((2,)), dma((2,)), dma((segs,)), dma((segs,)), dma((slabs,)), dma((slabs,)),
        ],
        compiler_params=pltpu.CompilerParams(collective_id=0, has_side_effects=True),
    )(pair_target, pair_source, junction_cell, junction_target, wall_near.transpose(0, 2, 1),
      positions.transpose(0, 2, 1, 3), density.transpose(0, 2, 1, 3), upsample, quad_weights, coarse_weights,
      wall_points, wall_traction)
    return result.transpose(0, 2, 1, 3)


def solution(mesh):
    placed = (
        P("seg", "slab", None, None),
        P("seg", "slab", None, None),
        P(),
        P(),
        P(),
        P("seg", "slab"),
        P("seg", "slab"),
        P("seg", "slab", None),
        P("seg", "slab", None),
        P("seg", "slab", None, None),
        P("seg", "slab", None, None),
        P("seg", "slab", None),
    )
    body = functools.partial(local, mesh.shape["seg"], mesh.shape["slab"])
    return jax.shard_map(
        body, mesh=mesh, in_specs=placed, out_specs=P("seg", "slab", None, None), check_vma=False
    )
```

```python
import functools
import math

import jax
import jax.numpy as jnp
from jax import lax
from jax.experimental import pallas as pl
from jax.experimental.pallas import tpu as pltpu
from jax.sharding import PartitionSpec as P

MESH = pl.DeviceIdType.MESH
HALO = 2
EPSILON2 = 0.05
WALL_GAIN = 3.0
LANES = 128
TERMS = 16
KAPPA = 1.0 / EPSILON2
F32 = jnp.float32
BF16 = jnp.bfloat16


def up(n, m):
    return -(-n // m) * m


def split(value, parts):
    out = []
    for _ in range(parts):
        piece = value.astype(BF16).astype(F32)
        out.append(piece)
        value = value - piece
    return out


def kernel(
    cfg,
    pair_target_far, pair_source_far, junction_cell_far, junction_target_far, wall_near_far,
    positions, density, upsample, quad_far, coarse_far, wall_points, wall_traction,
    out,
    pair_target, pair_source, junction_cell, junction_target, wall_near, quad, coarse,
    own, low, high, jsend, jrecv, walls, ups, rows, lhs, fine, ysrc, gsrc, yd, yg, ga, gb, xt, xs, wide, acc,
    local_sem, halo_send, halo_recv, junction_send, junction_recv, wall_send, wall_recv,
):
    count, points, fine_points, pairs, near, patch, segs, slabs, per_slab = cfg
    pt, qp = up(points, LANES), up(fine_points, LANES)
    rows_t = up(points, 16)
    seg, slab = lax.axis_index("seg"), lax.axis_index("slab")

    barrier = pltpu.get_barrier_semaphore()
    for o in range(1, segs):
        pl.semaphore_signal(barrier, inc=1, device_id={"seg": lax.rem(seg + o, segs)}, device_id_type=MESH)
    for o in range(1, slabs):
        pl.semaphore_signal(barrier, inc=1, device_id={"slab": lax.rem(slab + o, slabs)}, device_id_type=MESH)

    copies = [
        pltpu.make_async_copy(positions.at[0], own.at[0], local_sem.at[0]),
        pltpu.make_async_copy(density.at[0], own.at[1], local_sem.at[1]),
        pltpu.make_async_copy(wall_points.at[0], walls.at[pl.ds(slab * per_slab, per_slab), 0], local_sem.at[2]),
        pltpu.make_async_copy(wall_traction.at[0], walls.at[pl.ds(slab * per_slab, per_slab), 1], local_sem.at[3]),
    ]
    big = pltpu.make_async_copy(upsample, ups, local_sem.at[4])
    tables = [
        pltpu.make_async_copy(source, target, local_sem.at[5 + i]) for i, (source, target) in enumerate([
            (pair_target_far, pair_target), (pair_source_far, pair_source), (junction_cell_far, junction_cell),
            (junction_target_far, junction_target), (wall_near_far, wall_near), (quad_far, quad), (coarse_far, coarse)])
    ]
    for copy in copies + tables:
        copy.start()
    big.start()

    for copy in copies + tables:
        copy.wait()
    cell_at = lax.broadcasted_iota(jnp.int32, (count, points), 0)

    def pick(kind, i, near_by):
        total = jnp.zeros((count, points), F32)
        for ref, first in near_by:
            total = total + jnp.where(cell_at == first, ref[kind, i].astype(F32), 0.0)
        return jnp.sum(total, axis=0, keepdims=True)

    for b in range(segs):
        mine = junction_cell[0, 0, b]
        jsend[b] = jnp.concatenate(
            [pick(kind, i, [(own, mine)]) for kind in range(2) for i in range(3)], axis=0).astype(BF16)
    ysrc[...] = jnp.zeros_like(ysrc)
    gsrc[...] = jnp.zeros_like(gsrc)

    @pl.when(slab == 0)
    def _():
        low[...] = jnp.zeros_like(low)

    @pl.when(slab == slabs - 1)
    def _():
        high[...] = jnp.zeros_like(high)

    rows[...] = jnp.zeros_like(rows)
    coords = [own[0, i].astype(F32) for i in range(3)]
    norms = split(KAPPA * (coords[0] * coords[0] + coords[1] * coords[1] + coords[2] * coords[2]), 3)
    rows[9:12, 0:points] = jnp.ones((3, points), F32)
    def target_rows(c):
        for i in range(3):
            line = coords[i][c:c + 1]
            xs[c, i:i + 1] = line
            rows[i:i + 1, 0:points] = line
            rows[3 + i:4 + i, 0:points] = line
            rows[6 + i:7 + i, 0:points] = norms[i][c:c + 1]
        turned = rows[...].T[0:rows_t]
        xt[c] = turned.astype(BF16)
        for i in range(3):
            wide[c, i] = jnp.broadcast_to(turned[:, i:i + 1], (rows_t, LANES))
        acc[c] = jnp.zeros(acc.shape[1:], F32)

    for c in range(count // 2):
        target_rows(c)
    pl.semaphore_wait(barrier, segs - 1 + slabs - 1)

    def halo_up():
        return pltpu.make_async_remote_copy(
            own, low, halo_send.at[0], halo_recv.at[0],
            device_id={"slab": lax.rem(slab + 1, slabs)}, device_id_type=MESH)

    def halo_down():
        return pltpu.make_async_remote_copy(
            own, high, halo_send.at[1], halo_recv.at[1],
            device_id={"slab": lax.rem(slab + slabs - 1, slabs)}, device_id_type=MESH)

    def junction(o):
        return pltpu.make_async_remote_copy(
            jsend.at[lax.rem(seg + o, segs)], jrecv.at[seg], junction_send.at[o], junction_recv.at[o],
            device_id={"seg": lax.rem(seg + o, segs)}, device_id_type=MESH)

    def junction_in(o):
        return pltpu.make_async_remote_copy(
            jsend.at[seg], jrecv.at[lax.rem(seg + segs - o, segs)], junction_send.at[o], junction_recv.at[o],
            device_id={"seg": lax.rem(seg + o, segs)}, device_id_type=MESH)

    def wall(o, of):
        slot = pl.ds(of * per_slab, per_slab)
        return pltpu.make_async_remote_copy(
            walls.at[slot], walls.at[slot], wall_send.at[o], wall_recv.at[o],
            device_id={"slab": lax.rem(slab + o, slabs)}, device_id_type=MESH)

    @pl.when(slab < slabs - 1)
    def _():
        halo_up().start()

    @pl.when(slab > 0)
    def _():
        halo_down().start()

    for o in range(1, segs):
        junction(o).start()
    for o in range(slabs - 1, 0, -1):
        wall(o, slab).start()

    for c in range(count // 2, count):
        target_rows(c)

    def prepare(start, size):
        at = pl.ds(start, size)
        y, g = ysrc[0:3, at], gsrc[0:3, at]
        g_hi, g_lo = split(g, 2)
        y_hi, y_lo = split((-2.0 * KAPPA) * y, 2)
        norm = split(KAPPA * jnp.sum(y * y, axis=0, keepdims=True) + 1.0, 3)
        dot = -jnp.sum(y * (g_hi + g_lo), axis=0, keepdims=True)
        gsrc[0:3, at] = g_hi + g_lo
        gsrc[3:4, at] = dot
        dot = split(dot, 3)
        one = jnp.ones((3, size), F32)
        none = jnp.zeros((3, size), F32)
        pad = jnp.zeros((TERMS - 12, size), F32)
        yd[:, at] = jnp.concatenate([y_hi, y_lo, one] + norm + [pad], axis=0).astype(BF16)
        yg[:, at] = jnp.concatenate([g_hi, g_lo, none] + dot + [pad], axis=0).astype(BF16)
        ga[:, at] = jnp.concatenate([one[0:1], y, jnp.zeros((TERMS - 4, size), F32)], axis=0).astype(BF16)
        gb[:, at] = jnp.concatenate([jnp.zeros((TERMS - 8, size), F32), g_hi, g_lo, none[0:2]], axis=0).astype(BF16)

    def finish(distance, along, at):
        inverse = lax.rsqrt(distance)
        inverse3 = inverse * inverse * inverse
        return lax.dot_general(
            jnp.concatenate([ga[:, at], gb[:, at]], axis=1),
            jnp.concatenate([(along * inverse3).astype(BF16), (inverse + inverse3).astype(BF16)], axis=1),
            (((1,), (1,)), ((), ())), preferred_element_type=F32)

    def group(target, start, size):
        targets = xt[target]
        ats = [pl.ds(pl.multiple_of(start + i * LANES, LANES), LANES) for i in range(size)]
        total = None
        single = {7: 3, 6: 2}.get(size, size % 2)
        for i in range(0, size - single, 2):
            pair = jnp.dot(
                targets, jnp.concatenate([yd[:, ats[i]], yd[:, ats[i + 1]]], axis=1), preferred_element_type=F32)
            for at, distance in ((ats[i], pair[:, :LANES]), (ats[i + 1], pair[:, LANES:])):
                along = gsrc[3:4, at] + wide[target, 0] * gsrc[0:1, at]
                along = along + wide[target, 1] * gsrc[1:2, at]
                along = along + wide[target, 2] * gsrc[2:3, at]
                term = finish(distance, along, at)
                total = term if total is None else total + term
        for at in ats[size - single:]:
            both = jnp.dot(
                targets, jnp.concatenate([yd[:, at], yg[:, at]], axis=1), preferred_element_type=F32)
            term = finish(both[:, :LANES], both[:, LANES:], at)
            total = term if total is None else total + term
        return total

    def block(target, start, chunks):
        size = max(n for n in range(1, 8) if chunks % n == 0)

        def step(i, total):
            return total + group(target, start + i * size * LANES, size)

        if chunks == size:
            return group(target, start, size)
        return lax.fori_loop(0, chunks // size, step, jnp.zeros((TERMS, rows_t), F32))

    def add(target, value):
        for c in range(count):
            acc[c] = acc[c] + jnp.where(target == c, 1.0, 0.0) * value

    @pl.when(slab > 0)
    def _():
        halo_up().wait_recv()

    @pl.when(slab < slabs - 1)
    def _():
        halo_down().wait_recv()

    for k in range(pairs):
        source = pair_source[0, k]
        around = [(low, source + (count - HALO)), (own, source - HALO), (high, source - (HALO + count))]
        for kind in range(2):
            for i in range(3):
                lhs[6 * k + 3 * kind + i:6 * k + 3 * kind + i + 1] = pick(kind, i, around)
    big.wait()
    fine[...] = jnp.dot(lhs[...].astype(BF16), ups[...], preferred_element_type=F32).astype(BF16).astype(F32)
    for k in range(pairs):
        ysrc[0:3, pl.ds(k * qp, fine_points)] = fine[6 * k:6 * k + 3]
        gsrc[0:3, pl.ds(k * qp, fine_points)] = fine[6 * k + 3:6 * k + 6] * quad[...][None]
    prepare(0, pairs * qp)
    for k in range(pairs):
        target = pair_target[0, k]
        add(target, block(target, k * qp, qp // LANES))

    base = pairs * qp
    for o in range(1, segs):
        junction_in(o).wait_recv()
        source = jrecv[lax.rem(seg + segs - o, segs)]
        at = pl.ds(base + (o - 1) * pt, points)
        ysrc[0:3, at] = source[0:3].astype(F32)
        gsrc[0:3, at] = source[3:6].astype(F32) * coarse[...][None]
    prepare(base, (segs - 1) * pt)
    for o in range(1, segs):
        target = junction_target[0, 0, lax.rem(seg + segs - o, segs)]
        add(target, block(target, base + (o - 1) * pt, pt // LANES))

    base = base + (segs - 1) * pt
    for o in range(1, slabs):
        wall(o, lax.rem(slab + slabs - o, slabs)).wait_recv()
    width = up(patch, LANES)
    for c in range(count):
        for n in range(near):
            source = walls[wall_near[0, n, c]]
            at = pl.ds(base + (c * near + n) * width, patch)
            ysrc[0:3, at] = source[0].astype(F32)
            gsrc[0:3, at] = source[1].astype(F32) * WALL_GAIN
    prepare(base, count * near * width)
    scale = 1.0 / (math.sqrt(EPSILON2) * 8.0 * math.pi)
    for c in range(count):
        total = (acc[c] + block(c, base + c * near * width, near * width // LANES))[:, 0:points]
        x = xs[c, 0:3]
        value = scale * (total[8:11] + total[11:14] + KAPPA * (x * total[0:1] - total[1:4]))
        for i in range(3):
            out[0, i, c:c + 1] = value[i:i + 1]

    @pl.when(slab < slabs - 1)
    def _():
        halo_up().wait_send()

    @pl.when(slab > 0)
    def _():
        halo_down().wait_send()

    for o in range(1, segs):
        junction(o).wait_send()
    for o in range(1, slabs):
        wall(o, slab).wait_send()


def local(segs, slabs, positions, density, upsample, quad_weights, coarse_weights, pair_target, pair_source,
          junction_cell, junction_target, wall_points, wall_traction, wall_near):
    count, points = positions.shape[1], positions.shape[3]
    turned = (1, 3, count, points)
    fine_points = upsample.shape[1]
    pairs, near = pair_target.shape[1], wall_near.shape[2]
    per_slab, patch = wall_points.shape[1], wall_points.shape[3]
    cfg = (count, points, fine_points, pairs, near, patch, segs, slabs, per_slab)
    pt, qp = up(points, LANES), up(fine_points, LANES)
    lanes = pairs * qp + (segs - 1) * pt + count * near * up(patch, LANES)
    vmem = pl.BlockSpec(memory_space=pltpu.VMEM)
    far = pl.BlockSpec(memory_space=pl.ANY)
    dma = pltpu.SemaphoreType.DMA
    result = pl.pallas_call(
        functools.partial(kernel, cfg),
        out_shape=jax.ShapeDtypeStruct(turned, F32),
        in_specs=[far] * 12,
        out_specs=vmem,
        scratch_shapes=[
            pltpu.SMEM(pair_target.shape, jnp.int32),
            pltpu.SMEM(pair_source.shape, jnp.int32),
            pltpu.SMEM(junction_cell.shape, jnp.int32),
            pltpu.SMEM(junction_target.shape, jnp.int32),
            pltpu.SMEM((1, near, count), jnp.int32),
            pltpu.VMEM(quad_weights.shape, F32),
            pltpu.VMEM(coarse_weights.shape, F32),
            pltpu.VMEM((2,) + turned[1:], BF16),
            pltpu.VMEM((2,) + turned[1:], BF16),
            pltpu.VMEM((2,) + turned[1:], BF16),
            pltpu.VMEM((segs, 6, points), BF16),
            pltpu.VMEM((segs, 6, points), BF16),
            pltpu.VMEM((slabs * per_slab, 2, 3, patch), BF16),
            pltpu.VMEM(upsample.shape, BF16),
            pltpu.VMEM((TERMS, pt), F32),
            pltpu.VMEM((6 * pairs, points), F32),
            pltpu.VMEM((6 * pairs, fine_points), F32),
            pltpu.VMEM((8, lanes), F32),
            pltpu.VMEM((8, lanes), F32),
            pltpu.VMEM((TERMS, lanes), BF16),
            pltpu.VMEM((TERMS, lanes), BF16),
            pltpu.VMEM((TERMS, lanes), BF16),
            pltpu.VMEM((TERMS, lanes), BF16),
            pltpu.VMEM((count, up(points, 16), TERMS), BF16),
            pltpu.VMEM((count, 3, points), F32),
            pltpu.VMEM((count, 3, up(points, 16), LANES), F32),
            pltpu.VMEM((count, TERMS, up(points, 16)), F32),
            dma((12,)), dma((2,)), dma((2,)), dma((segs,)), dma((segs,)), dma((slabs,)), dma((slabs,)),
        ],
        compiler_params=pltpu.CompilerParams(collective_id=0, has_side_effects=True),
    )(pair_target, pair_source, junction_cell, junction_target, wall_near.transpose(0, 2, 1),
      positions.transpose(0, 2, 1, 3), density.transpose(0, 2, 1, 3), upsample, quad_weights, coarse_weights,
      wall_points, wall_traction)
    return result.transpose(0, 2, 1, 3)


def solution(mesh):
    placed = (
        P("seg", "slab", None, None),
        P("seg", "slab", None, None),
        P(),
        P(),
        P(),
        P("seg", "slab"),
        P("seg", "slab"),
        P("seg", "slab", None),
        P("seg", "slab", None),
        P("seg", "slab", None, None),
        P("seg", "slab", None, None),
        P("seg", "slab", None),
    )
    body = functools.partial(local, mesh.shape["seg"], mesh.shape["slab"])
    return jax.shard_map(
        body, mesh=mesh, in_specs=placed, out_specs=P("seg", "slab", None, None), check_vma=False
    )
```

```python
import functools
import math

import jax
import jax.numpy as jnp
from jax import lax
from jax.experimental import pallas as pl
from jax.experimental.pallas import tpu as pltpu
from jax.sharding import PartitionSpec as P

MESH = pl.DeviceIdType.MESH
HALO = 2
EPSILON2 = 0.05
WALL_GAIN = 3.0
LANES = 128
TERMS = 16
MOST = 7
KAPPA = 1.0 / EPSILON2
F32 = jnp.float32
BF16 = jnp.bfloat16


def up(n, m):
    return -(-n // m) * m


def split(value, parts):
    out = []
    for _ in range(parts):
        piece = value.astype(BF16).astype(F32)
        out.append(piece)
        value = value - piece
    return out


def kernel(
    cfg,
    pair_target_far, pair_source_far, junction_cell_far, junction_target_far, wall_near_far,
    positions, density, upsample, quad_far, coarse_far, wall_points, wall_traction,
    out,
    pair_target, pair_source, junction_cell, junction_target, wall_near, quad, coarse,
    own, low, high, jsend, jrecv, walls, ups, rows, lhs, fine, ysrc, gsrc, yd, yg, ga, gb, xt, xs, wide, acc,
    local_sem, halo_send, halo_recv, junction_send, junction_recv, wall_send, wall_recv,
):
    count, points, fine_points, pairs, near, patch, segs, slabs, per_slab = cfg
    pt, qp = up(points, LANES), up(fine_points, LANES)
    rows_t = up(points, 16)
    seg, slab = lax.axis_index("seg"), lax.axis_index("slab")

    barrier = pltpu.get_barrier_semaphore()
    for o in range(1, segs):
        pl.semaphore_signal(barrier, inc=1, device_id={"seg": lax.rem(seg + o, segs)}, device_id_type=MESH)
    for o in range(1, slabs):
        pl.semaphore_signal(barrier, inc=1, device_id={"slab": lax.rem(slab + o, slabs)}, device_id_type=MESH)

    copies = [
        pltpu.make_async_copy(positions.at[0], own.at[0], local_sem.at[0]),
        pltpu.make_async_copy(density.at[0], own.at[1], local_sem.at[1]),
        pltpu.make_async_copy(wall_points.at[0], walls.at[pl.ds(slab * per_slab, per_slab), 0], local_sem.at[2]),
        pltpu.make_async_copy(wall_traction.at[0], walls.at[pl.ds(slab * per_slab, per_slab), 1], local_sem.at[3]),
    ]
    big = pltpu.make_async_copy(upsample, ups, local_sem.at[4])
    tables = [
        pltpu.make_async_copy(source, target, local_sem.at[5 + i]) for i, (source, target) in enumerate([
            (pair_target_far, pair_target), (pair_source_far, pair_source), (junction_cell_far, junction_cell),
            (junction_target_far, junction_target), (wall_near_far, wall_near), (quad_far, quad), (coarse_far, coarse)])
    ]
    for copy in copies + tables:
        copy.start()
    big.start()

    for copy in copies + tables:
        copy.wait()
    cell_at = lax.broadcasted_iota(jnp.int32, (count, points), 0)

    def pick(kind, i, near_by):
        total = jnp.zeros((count, points), F32)
        for ref, first in near_by:
            total = total + jnp.where(cell_at == first, ref[kind, i].astype(F32), 0.0)
        return jnp.sum(total, axis=0, keepdims=True)

    for b in range(segs):
        mine = junction_cell[0, 0, b]
        jsend[b] = jnp.concatenate(
            [pick(kind, i, [(own, mine)]) for kind in range(2) for i in range(3)], axis=0).astype(BF16)
    ysrc[...] = jnp.zeros_like(ysrc)
    gsrc[...] = jnp.zeros_like(gsrc)

    @pl.when(slab == 0)
    def _():
        low[...] = jnp.zeros_like(low)

    @pl.when(slab == slabs - 1)
    def _():
        high[...] = jnp.zeros_like(high)

    rows[...] = jnp.zeros_like(rows)
    coords = [own[0, i].astype(F32) for i in range(3)]
    norms = split(KAPPA * (coords[0] * coords[0] + coords[1] * coords[1] + coords[2] * coords[2]), 3)
    rows[9:12, 0:points] = jnp.ones((3, points), F32)
    def target_rows(c):
        for i in range(3):
            line = coords[i][c:c + 1]
            xs[c, i:i + 1] = line
            rows[i:i + 1, 0:points] = line
            rows[3 + i:4 + i, 0:points] = line
            rows[6 + i:7 + i, 0:points] = norms[i][c:c + 1]
        turned = rows[...].T[0:rows_t]
        xt[c] = turned.astype(BF16)
        for i in range(3):
            wide[c, i] = jnp.broadcast_to(turned[:, i:i + 1], (rows_t, LANES))
        acc[c] = jnp.zeros(acc.shape[1:], F32)

    for c in range(count // 2):
        target_rows(c)
    pl.semaphore_wait(barrier, segs - 1 + slabs - 1)

    def halo_up():
        return pltpu.make_async_remote_copy(
            own, low, halo_send.at[0], halo_recv.at[0],
            device_id={"slab": lax.rem(slab + 1, slabs)}, device_id_type=MESH)

    def halo_down():
        return pltpu.make_async_remote_copy(
            own, high, halo_send.at[1], halo_recv.at[1],
            device_id={"slab": lax.rem(slab + slabs - 1, slabs)}, device_id_type=MESH)

    def junction(o):
        return pltpu.make_async_remote_copy(
            jsend.at[lax.rem(seg + o, segs)], jrecv.at[seg], junction_send.at[o], junction_recv.at[o],
            device_id={"seg": lax.rem(seg + o, segs)}, device_id_type=MESH)

    def junction_in(o):
        return pltpu.make_async_remote_copy(
            jsend.at[seg], jrecv.at[lax.rem(seg + segs - o, segs)], junction_send.at[o], junction_recv.at[o],
            device_id={"seg": lax.rem(seg + o, segs)}, device_id_type=MESH)

    def wall(o, of):
        slot = pl.ds(of * per_slab, per_slab)
        return pltpu.make_async_remote_copy(
            walls.at[slot], walls.at[slot], wall_send.at[o], wall_recv.at[o],
            device_id={"slab": lax.rem(slab + o, slabs)}, device_id_type=MESH)

    @pl.when(slab < slabs - 1)
    def _():
        halo_up().start()

    @pl.when(slab > 0)
    def _():
        halo_down().start()

    for o in range(1, segs):
        junction(o).start()
    for o in range(slabs - 1, 0, -1):
        wall(o, slab).start()

    for c in range(count // 2, count):
        target_rows(c)

    def prepare(start, size):
        at = pl.ds(start, size)
        y, g = ysrc[0:3, at], gsrc[0:3, at]
        g_hi, g_lo = split(g, 2)
        y_hi, y_lo = split((-2.0 * KAPPA) * y, 2)
        norm = split(KAPPA * jnp.sum(y * y, axis=0, keepdims=True) + 1.0, 3)
        dot = -jnp.sum(y * (g_hi + g_lo), axis=0, keepdims=True)
        gsrc[0:3, at] = g_hi + g_lo
        gsrc[3:4, at] = dot
        dot = split(dot, 3)
        one = jnp.ones((3, size), F32)
        none = jnp.zeros((3, size), F32)
        pad = jnp.zeros((TERMS - 12, size), F32)
        yd[:, at] = jnp.concatenate([y_hi, y_lo, one] + norm + [pad], axis=0).astype(BF16)
        yg[:, at] = jnp.concatenate([g_hi, g_lo, none] + dot + [pad], axis=0).astype(BF16)
        ga[:, at] = jnp.concatenate([one[0:1], y, jnp.zeros((TERMS - 4, size), F32)], axis=0).astype(BF16)
        gb[:, at] = jnp.concatenate([jnp.zeros((TERMS - 8, size), F32), g_hi, g_lo, none[0:2]], axis=0).astype(BF16)

    def finish(distance, along, at):
        inverse = lax.rsqrt(distance)
        inverse3 = inverse * inverse * inverse
        return lax.dot_general(
            jnp.concatenate([ga[:, at], gb[:, at]], axis=1),
            jnp.concatenate([(along * inverse3).astype(BF16), (inverse + inverse3).astype(BF16)], axis=1),
            (((1,), (1,)), ((), ())), preferred_element_type=F32)

    def group(target, start, size):
        targets = xt[target]
        ats = [pl.ds(pl.multiple_of(start + i * LANES, LANES), LANES) for i in range(size)]
        total = None
        single = {7: 3, 6: 2}.get(size, size % 2)
        for i in range(0, size - single, 2):
            pair = jnp.dot(
                targets, jnp.concatenate([yd[:, ats[i]], yd[:, ats[i + 1]]], axis=1), preferred_element_type=F32)
            for at, distance in ((ats[i], pair[:, :LANES]), (ats[i + 1], pair[:, LANES:])):
                along = gsrc[3:4, at] + wide[target, 0] * gsrc[0:1, at]
                along = along + wide[target, 1] * gsrc[1:2, at]
                along = along + wide[target, 2] * gsrc[2:3, at]
                term = finish(distance, along, at)
                total = term if total is None else total + term
        for at in ats[size - single:]:
            both = jnp.dot(
                targets, jnp.concatenate([yd[:, at], yg[:, at]], axis=1), preferred_element_type=F32)
            term = finish(both[:, :LANES], both[:, LANES:], at)
            total = term if total is None else total + term
        return total

    def block(target, start, chunks):
        size = max(n for n in range(1, 8) if chunks % n == 0)

        def step(i, total):
            return total + group(target, start + i * size * LANES, size)

        if chunks == size:
            return group(target, start, size)
        return lax.fori_loop(0, chunks // size, step, jnp.zeros((TERMS, rows_t), F32))

    def add(target, value):
        for c in range(count):
            acc[c] = acc[c] + jnp.where(target == c, 1.0, 0.0) * value

    @pl.when(slab > 0)
    def _():
        halo_up().wait_recv()

    @pl.when(slab < slabs - 1)
    def _():
        halo_down().wait_recv()

    for k in range(pairs):
        source = pair_source[0, k]
        around = [(low, source + (count - HALO)), (own, source - HALO), (high, source - (HALO + count))]
        for kind in range(2):
            for i in range(3):
                lhs[6 * k + 3 * kind + i:6 * k + 3 * kind + i + 1] = pick(kind, i, around)
    big.wait()
    fine[...] = jnp.dot(lhs[...].astype(BF16), ups[...], preferred_element_type=F32).astype(BF16).astype(F32)
    for k in range(pairs):
        ysrc[0:3, pl.ds(k * qp, fine_points)] = fine[6 * k:6 * k + 3]
        gsrc[0:3, pl.ds(k * qp, fine_points)] = fine[6 * k + 3:6 * k + 6] * quad[...][None]
    prepare(0, pairs * qp)
    size = max(n for n in range(1, MOST + 1) if (qp // LANES) % n == 0)

    def together(i, totals):
        return tuple(
            total + group(pair_target[0, k], k * qp + i * size * LANES, size) for k, total in enumerate(totals))

    zero = jnp.zeros((TERMS, rows_t), F32)
    totals = lax.fori_loop(0, qp // LANES // size, together, (zero,) * pairs)
    for k in range(pairs):
        add(pair_target[0, k], totals[k])

    base = pairs * qp
    for o in range(1, segs):
        junction_in(o).wait_recv()
        source = jrecv[lax.rem(seg + segs - o, segs)]
        at = pl.ds(base + (o - 1) * pt, points)
        ysrc[0:3, at] = source[0:3].astype(F32)
        gsrc[0:3, at] = source[3:6].astype(F32) * coarse[...][None]
    prepare(base, (segs - 1) * pt)
    for o in range(1, segs):
        target = junction_target[0, 0, lax.rem(seg + segs - o, segs)]
        add(target, block(target, base + (o - 1) * pt, pt // LANES))

    base = base + (segs - 1) * pt
    for o in range(1, slabs):
        wall(o, lax.rem(slab + slabs - o, slabs)).wait_recv()
    width = up(patch, LANES)
    for c in range(count):
        for n in range(near):
            source = walls[wall_near[0, n, c]]
            at = pl.ds(base + (c * near + n) * width, patch)
            ysrc[0:3, at] = source[0].astype(F32)
            gsrc[0:3, at] = source[1].astype(F32) * WALL_GAIN
    prepare(base, count * near * width)
    scale = 1.0 / (math.sqrt(EPSILON2) * 8.0 * math.pi)
    for c in range(count):
        total = (acc[c] + block(c, base + c * near * width, near * width // LANES))[:, 0:points]
        x = xs[c, 0:3]
        value = scale * (total[8:11] + total[11:14] + KAPPA * (x * total[0:1] - total[1:4]))
        for i in range(3):
            out[0, i, c:c + 1] = value[i:i + 1]

    @pl.when(slab < slabs - 1)
    def _():
        halo_up().wait_send()

    @pl.when(slab > 0)
    def _():
        halo_down().wait_send()

    for o in range(1, segs):
        junction(o).wait_send()
    for o in range(1, slabs):
        wall(o, slab).wait_send()


def local(segs, slabs, positions, density, upsample, quad_weights, coarse_weights, pair_target, pair_source,
          junction_cell, junction_target, wall_points, wall_traction, wall_near):
    count, points = positions.shape[1], positions.shape[3]
    turned = (1, 3, count, points)
    fine_points = upsample.shape[1]
    pairs, near = pair_target.shape[1], wall_near.shape[2]
    per_slab, patch = wall_points.shape[1], wall_points.shape[3]
    cfg = (count, points, fine_points, pairs, near, patch, segs, slabs, per_slab)
    pt, qp = up(points, LANES), up(fine_points, LANES)
    lanes = pairs * qp + (segs - 1) * pt + count * near * up(patch, LANES)
    vmem = pl.BlockSpec(memory_space=pltpu.VMEM)
    far = pl.BlockSpec(memory_space=pl.ANY)
    dma = pltpu.SemaphoreType.DMA
    result = pl.pallas_call(
        functools.partial(kernel, cfg),
        out_shape=jax.ShapeDtypeStruct(turned, F32),
        in_specs=[far] * 12,
        out_specs=vmem,
        scratch_shapes=[
            pltpu.SMEM(pair_target.shape, jnp.int32),
            pltpu.SMEM(pair_source.shape, jnp.int32),
            pltpu.SMEM(junction_cell.shape, jnp.int32),
            pltpu.SMEM(junction_target.shape, jnp.int32),
            pltpu.SMEM((1, near, count), jnp.int32),
            pltpu.VMEM(quad_weights.shape, F32),
            pltpu.VMEM(coarse_weights.shape, F32),
            pltpu.VMEM((2,) + turned[1:], BF16),
            pltpu.VMEM((2,) + turned[1:], BF16),
            pltpu.VMEM((2,) + turned[1:], BF16),
            pltpu.VMEM((segs, 6, points), BF16),
            pltpu.VMEM((segs, 6, points), BF16),
            pltpu.VMEM((slabs * per_slab, 2, 3, patch), BF16),
            pltpu.VMEM(upsample.shape, BF16),
            pltpu.VMEM((TERMS, pt), F32),
            pltpu.VMEM((6 * pairs, points), F32),
            pltpu.VMEM((6 * pairs, fine_points), F32),
            pltpu.VMEM((8, lanes), F32),
            pltpu.VMEM((8, lanes), F32),
            pltpu.VMEM((TERMS, lanes), BF16),
            pltpu.VMEM((TERMS, lanes), BF16),
            pltpu.VMEM((TERMS, lanes), BF16),
            pltpu.VMEM((TERMS, lanes), BF16),
            pltpu.VMEM((count, up(points, 16), TERMS), BF16),
            pltpu.VMEM((count, 3, points), F32),
            pltpu.VMEM((count, 3, up(points, 16), LANES), F32),
            pltpu.VMEM((count, TERMS, up(points, 16)), F32),
            dma((12,)), dma((2,)), dma((2,)), dma((segs,)), dma((segs,)), dma((slabs,)), dma((slabs,)),
        ],
        compiler_params=pltpu.CompilerParams(collective_id=0, has_side_effects=True),
    )(pair_target, pair_source, junction_cell, junction_target, wall_near.transpose(0, 2, 1),
      positions.transpose(0, 2, 1, 3), density.transpose(0, 2, 1, 3), upsample, quad_weights, coarse_weights,
      wall_points, wall_traction)
    return result.transpose(0, 2, 1, 3)


def solution(mesh):
    placed = (
        P("seg", "slab", None, None),
        P("seg", "slab", None, None),
        P(),
        P(),
        P(),
        P("seg", "slab"),
        P("seg", "slab"),
        P("seg", "slab", None),
        P("seg", "slab", None),
        P("seg", "slab", None, None),
        P("seg", "slab", None, None),
        P("seg", "slab", None),
    )
    body = functools.partial(local, mesh.shape["seg"], mesh.shape["slab"])
    return jax.shard_map(
        body, mesh=mesh, in_specs=placed, out_specs=P("seg", "slab", None, None), check_vma=False
    )
```
